32 devices in a mesh: seq: 8 (over y, x, core), tensor: 4 (over z).
Axes of the slice: x: 2, y: 2, z: 4, core: 2. Of those that a mesh axis runs over, the one named last changes fastest.
Arguments:
- tokens: bfloat16 [4096, 2048], P('seq'), may hold values from -200 to 200
- w_latent: bfloat16 [2048, 512], P(None, 'tensor'), may hold values from -0.125 to 0.125
- w_query: bfloat16 [2048, 2048], P(None, 'tensor'), may hold values from -0.125 to 0.125
- w_key_up: bfloat16 [512, 2048], P(None, 'tensor'), may hold values from -0.25 to 0.25
- w_value_up: bfloat16 [512, 2048], P(None, 'tensor'), may hold values from -0.25 to 0.25
- w_stu_query: bfloat16 [2048, 2048], P(None, 'tensor'), may hold values from -0.125 to 0.125
- w_stu_key: bfloat16 [2048, 2048], P(None, 'tensor'), may hold values from -0.125 to 0.125
- w_stu_value: bfloat16 [2048, 2048], P(None, 'tensor'), may hold values from -0.125 to 0.125
- forget: float32 [4096, 16], P('seq', 'tensor'), may hold values from -1 to 0
Outputs:
- teacher_out: bfloat16 [4096, 2048], P('seq', 'tensor')
- loss_mean: float32 [], replicated
- weight_grad: float32 [2048, 2048], P('seq', 'tensor')
The draws below stay inside these ranges and needn't reach their ends.
All inputs are finite; a program needn't handle non-finite values.
Results may differ from the reference program's by a relative error of at most 0.02.
The reference program's roundings to bfloat16 on the way (of `latent`, `queries`, `weights` and `value_grad`) count: a program that leaves them out, or rounds other values in their place, can miss the bound.
Values may be sent and summed in bfloat16 or wider, within the bound.
A program may use at most 64 MiB of HBM per device.

```python
import math
import jax
import jax.numpy as jnp
from jax import lax

D = 2048
HEAD_COUNT = 16
DH = 128
LAT = 512
TOK_DEV = 512
TOKEN_COUNT = 4096


def draw_tokens(key, part):
    base = jax.random.truncated_normal(jax.random.fold_in(key, 11), -6.0, 6.0, (TOKEN_COUNT, D), jnp.float32)
    return base.astype(jnp.bfloat16)


def draw_forget(key, part):
    keep_share = 0.5
    slow_heads = jax.random.uniform(jax.random.fold_in(key, 21), (1, HEAD_COUNT), jnp.float32) < keep_share
    slow_rate = jnp.exp(jax.random.uniform(jax.random.fold_in(key, 22), (1, HEAD_COUNT), jnp.float32, math.log(0.03), math.log(0.15))) / TOKEN_COUNT
    fast_rate = jnp.exp(jax.random.uniform(jax.random.fold_in(key, 23), (1, HEAD_COUNT), jnp.float32, math.log(1.0 / 50.0), math.log(1.0 / 30.0)))
    head_decay_rate = jnp.where(slow_heads, slow_rate, fast_rate)
    random_perturbation = jnp.exp(jax.random.uniform(jax.random.fold_in(key, 24), (TOKEN_COUNT, HEAD_COUNT), jnp.float32, math.log(0.5), math.log(2.0)))
    block_scale = jnp.exp(jax.random.uniform(jax.random.fold_in(key, 25), (TOKEN_COUNT // TOK_DEV, HEAD_COUNT), jnp.float32, math.log(0.5), math.log(2.0)))
    block_multiplier = jnp.repeat(block_scale, TOK_DEV, axis=0)
    episodes = jax.random.uniform(jax.random.fold_in(key, 26), (TOKEN_COUNT, 1), jnp.float32) < 3.0 / TOKEN_COUNT
    episode_loss = jnp.log(jax.random.uniform(jax.random.fold_in(key, 27), (TOKEN_COUNT, HEAD_COUNT), jnp.float32, 0.5, 0.8))
    return -(head_decay_rate * random_perturbation * block_multiplier) + jnp.where(episodes, episode_loss, 0.0)


def shard_levels(own_key, dims, split, least, largest):
    factor_of, own = 1.0, jax.random.fold_in(own_key, 6)
    for axis_at, parts in split:
        steps = jnp.exp(jax.random.uniform(jax.random.fold_in(own, axis_at), (parts,), jnp.float32, least / len(split), largest / len(split)))
        factor_of = factor_of * jnp.repeat(steps, dims[axis_at] // parts).reshape([-1 if axis == axis_at else 1 for axis in range(len(dims))])
    return factor_of


def normal_values(rng, dims, spread, bound, pieces=(), held_as=jnp.bfloat16):
    entries = spread * jax.random.normal(rng, dims, jnp.float32)
    if pieces:
        entries = entries * shard_levels(rng, dims, pieces, -0.22, 0.18)
    return jnp.clip(entries, -bound, bound).astype(held_as)


def setup_inputs(seed: int = 0) -> dict:
    seeds = jax.random.split(jax.random.key(seed), 10)
    tokens = draw_tokens(jax.random.fold_in(seeds[9], 71), 0)
    w_latent = normal_values(seeds[1], (D, LAT), D ** -0.5, 0.125, ((1, 4),))
    w_query = normal_values(seeds[2], (D, HEAD_COUNT * DH), D ** -0.5, 0.125, ((1, 4),))
    w_key_up = normal_values(seeds[3], (LAT, HEAD_COUNT * DH), LAT ** -0.5, 0.25, ((1, 4),))
    w_value_up = normal_values(seeds[4], (LAT, HEAD_COUNT * DH), LAT ** -0.5, 0.25, ((1, 4),))
    w_stu_query = normal_values(seeds[5], (D, HEAD_COUNT * DH), D ** -0.5, 0.125, ((1, 4),))
    w_stu_key = normal_values(seeds[6], (D, HEAD_COUNT * DH), D ** -0.5, 0.125, ((1, 4),))
    w_stu_value = normal_values(seeds[7], (D, HEAD_COUNT * DH), D ** -0.5, 0.125, ((1, 4),))
    forget = draw_forget(jax.random.fold_in(seeds[9], 71), 0)
    return {"tokens": tokens, "w_latent": w_latent, "w_query": w_query, "w_key_up": w_key_up, "w_value_up": w_value_up, "w_stu_query": w_stu_query, "w_stu_key": w_stu_key, "w_stu_value": w_stu_value, "forget": forget}


NEG_FILL = -1e+30
EPSILON = 1e-06

def split_heads(matrix):
    return matrix.reshape(matrix.shape[0], HEAD_COUNT, DH)

def unit_rows(matrix):
    return matrix * lax.rsqrt(lax.optimization_barrier(jnp.sum(matrix * matrix, axis=-1, keepdims=True)) + EPSILON)

def reference(tokens, w_latent, w_query, w_key_up, w_value_up, w_stu_query, w_stu_key, w_stu_value, forget):
    highest = lax.Precision.HIGHEST
    latent = jnp.dot(tokens, w_latent, preferred_element_type=jnp.float32).astype(jnp.bfloat16)
    queries = jnp.dot(tokens, w_query, preferred_element_type=jnp.float32).astype(jnp.bfloat16)
    keys = jnp.dot(latent, w_key_up, preferred_element_type=jnp.float32).astype(jnp.bfloat16)
    values = jnp.dot(latent, w_value_up, preferred_element_type=jnp.float32).astype(jnp.bfloat16)
    query_all = split_heads(queries.astype(jnp.float32))
    key_all = split_heads(keys.astype(jnp.float32))
    value_all = split_heads(values.astype(jnp.float32))
    block_size = math.gcd(TOKEN_COUNT, 512)
    block_count = TOKEN_COUNT // block_size
    score_scale = 1.0 / math.sqrt(DH)
    every_pos = jnp.arange(TOKEN_COUNT, dtype=jnp.int32)
    block_ids = jnp.arange(block_count, dtype=jnp.int32)

    def teacher_block(block_index):
        first_row = (block_index * block_size).astype(jnp.int32)
        query_part = lax.dynamic_slice_in_dim(query_all, first_row, block_size, 0)
        scores = jnp.einsum('qhd,khd->hqk', query_part, key_all) * score_scale
        positions = first_row + jnp.arange(block_size, dtype=jnp.int32)
        allowed = every_pos[None, :] <= positions[:, None]
        scores = jnp.where(allowed[None], scores, NEG_FILL)
        row_top = lax.optimization_barrier(jnp.max(scores, axis=2, keepdims=True))
        expos = jnp.where(allowed[None], jnp.exp(scores - row_top), 0.0)
        row_total = lax.optimization_barrier(jnp.sum(expos, axis=2))
        weights = expos.astype(jnp.bfloat16).astype(jnp.float32)
        mixed = jnp.einsum('hqk,khd->qhd', weights, value_all) / row_total.T[:, :, None]
        return mixed.reshape(block_size, HEAD_COUNT * DH).astype(jnp.bfloat16)
    teacher_out = lax.map(teacher_block, block_ids).reshape(TOKEN_COUNT, HEAD_COUNT * DH)
    stu_query = unit_rows(split_heads(jnp.dot(tokens, w_stu_query, preferred_element_type=jnp.float32)))
    stu_key = unit_rows(split_heads(jnp.dot(tokens, w_stu_key, preferred_element_type=jnp.float32)))
    stu_value = split_heads(jnp.dot(tokens, w_stu_value, preferred_element_type=jnp.float32))
    cumul = jnp.cumsum(forget, axis=0)

    def student_block(block_index):
        first_row = (block_index * block_size).astype(jnp.int32)
        query_part = lax.dynamic_slice_in_dim(stu_query, first_row, block_size, 0)
        cumul_part = lax.dynamic_slice_in_dim(cumul, first_row, block_size, 0)
        positions = first_row + jnp.arange(block_size, dtype=jnp.int32)
        allowed = every_pos[None, :] <= positions[:, None]
        scores = jnp.einsum('qhd,khd->hqk', query_part, stu_key, precision=highest)
        log_gap = cumul_part.T[:, :, None] - cumul.T[:, None, :]
        decays = jnp.exp(jnp.where(allowed[None], log_gap, NEG_FILL))
        return jnp.einsum('hqk,khd->qhd', scores * decays, stu_value, precision=highest)
    student_out = lax.map(student_block, block_ids).reshape(TOKEN_COUNT, HEAD_COUNT, DH)
    mismatch = student_out - split_heads(teacher_out.astype(jnp.float32))
    loss_mean = jnp.sum(mismatch * mismatch) / (2.0 * TOKEN_COUNT * HEAD_COUNT * DH)
    grad_out = mismatch / math.sqrt(TOKEN_COUNT)

    def value_block(block_index):
        first_row = (block_index * block_size).astype(jnp.int32)
        key_part = lax.dynamic_slice_in_dim(stu_key, first_row, block_size, 0)
        cumul_part = lax.dynamic_slice_in_dim(cumul, first_row, block_size, 0)
        positions = first_row + jnp.arange(block_size, dtype=jnp.int32)
        allowed = positions[:, None] <= every_pos[None, :]
        scores = jnp.einsum('khd,qhd->hkq', key_part, stu_query, precision=highest)
        log_gap = cumul.T[:, None, :] - cumul_part.T[:, :, None]
        decays = jnp.exp(jnp.where(allowed[None], log_gap, NEG_FILL))
        return jnp.einsum('hkq,qhd->khd', scores * decays, grad_out, precision=highest)
    value_grad = lax.map(value_block, block_ids).reshape(TOKEN_COUNT, HEAD_COUNT * DH).astype(jnp.bfloat16)
    weight_grad = jnp.dot(tokens.T, value_grad, preferred_element_type=jnp.float32)
    return (teacher_out, loss_mean, weight_grad)
```

```python
import functools
import math

import jax
import jax.numpy as jnp
from jax import lax
from jax.experimental import pallas as pl
from jax.experimental.pallas import tpu as pltpu
from jax.sharding import PartitionSpec as P

NEG_FILL = -1e30
EPSILON = 1e-06
MESH = pl.DeviceIdType.MESH
F32, BF16 = jnp.float32, jnp.bfloat16


def flip(index, mask):
    out, bit = index, 0
    while (1 << bit) <= mask:
        if (mask >> bit) & 1:
            out = out + (1 << bit) * (1 - 2 * ((index // (1 << bit)) % 2))
        bit += 1
    return out


def combos(bits):
    out = [0]
    for b in bits:
        out = out + [o | (1 << b) for o in out]
    return out


def dot_t(a, b):
    return lax.dot_general(a, b, (((1,), (1,)), ((), ())), preferred_element_type=F32)


def dot(a, b):
    return jnp.dot(a, b, preferred_element_type=F32)


def kernel(
    n, nt, heads, hs, rows,
    tok_h, wl_h, wq_h, wku_h, wvu_h, wsq_h, wsk_h, wsv_h, crow_ref, ccol_ref,
    tout_ref, loss_ref, wg_ref,
    tok, wl, wq, wku, wvu, wsq, wsk, wsv, wvut,
    parts, lat, q_s, sq_s, sk_s, svt, mix, out_t, m_s, l_s, acc_s,
    st_own, st_pre, st_send, st_recv, lt_send, lt_recv,
    gt, bt_own, bt_suf, bt_send, bt_recv, vgt,
    wg_acc, wg_send, wg_recv, loss_t, loss_r, loss_s, loss_r2,
    ld_sem, part_ss, part_rs, lat_ss, lat_rs, st_ss, st_rs, lt_ss, lt_rs, bt_ss, bt_rs,
    wg_ss, wg_rs, lo_ss, lo_rs, lp_ss, lp_rs,
):
    me = lax.axis_index("seq")
    tme = lax.axis_index("tensor")
    nb = n.bit_length() - 1
    scale = math.log2(math.e) / math.sqrt(hs)

    def bit_of(b):
        return (me // (1 << b)) % 2

    loads = [
        pltpu.make_async_copy(src, dst, ld_sem.at[i])
        for i, (src, dst) in enumerate(
            [(tok_h, tok), (wl_h, wl), (wsk_h, wsk), (wsv_h, wsv), (wsq_h, wsq), (wq_h, wq), (wku_h, wku), (wvu_h, wvu)]
        )
    ]
    for load in loads:
        load.start()

    barrier = pltpu.get_barrier_semaphore()
    for b in range(nb):
        pl.semaphore_signal(barrier, inc=1, device_id=(flip(me, 1 << b), tme), device_id_type=MESH)
    for d in range(1, nt):
        pl.semaphore_signal(barrier, inc=1, device_id=(me, (tme + d) % nt), device_id_type=MESH)
    pl.semaphore_wait(barrier, nb + nt - 1)

    def seq_copy(src, dst, ss, rs, b):
        return pltpu.make_async_remote_copy(
            src_ref=src, dst_ref=dst, send_sem=ss, recv_sem=rs,
            device_id=(flip(me, 1 << b), tme), device_id_type=MESH,
        )

    def tensor_copy(src, dst, ss, rs, d):
        return pltpu.make_async_remote_copy(
            src_ref=src, dst_ref=dst, send_sem=ss, recv_sem=rs,
            device_id=(me, (tme + d) % nt), device_id_type=MESH,
        )

    pending = []

    loads[0].wait()
    loads[1].wait()
    parts[tme] = dot(tok[...], wl[...]).astype(BF16)
    part_copies = [
        tensor_copy(parts.at[tme], parts.at[tme], part_ss.at[d - 1], part_rs.at[d - 1], d) for d in range(1, nt)
    ]
    for c in part_copies:
        c.start()

    def unit(x):
        return x * lax.rsqrt(jnp.sum(x * x, axis=-1, keepdims=True) + EPSILON)

    loads[2].wait()
    x = dot(tok[...], wsk[...])
    for h in range(heads):
        sk_s[h] = unit(x[:, h * hs : (h + 1) * hs]).astype(BF16)
    loads[3].wait()
    x = dot(tok[...], wsv[...])
    lt = []
    for h in range(heads):
        xt = x[:, h * hs : (h + 1) * hs].T
        svt[h] = xt.astype(BF16)
        c_h = crow_ref[h : h + 1, :]
        end = c_h[:, rows - 1 : rows]
        st_own[h] = dot((xt * jnp.exp(end - c_h)).astype(BF16), sk_s[h])
        st_pre[h] = jnp.zeros((hs, hs), F32)
        lt.append(jnp.broadcast_to(end, (1, 128)))
    zero_row = jnp.zeros((1, 128), F32)
    lt_tile = jnp.concatenate(lt + [zero_row] * (8 - heads), axis=0)
    lp_tile = jnp.zeros((8, 128), F32)
    lr_tile = jnp.zeros((8, 128), F32)
    lt_hist = []

    def scan_start(s, own, send, recv, ss, rs):
        for h in range(heads):
            send[s, h] = own[h].astype(BF16)
        c = seq_copy(send.at[s], recv.at[s], ss.at[s], rs.at[s], s)
        c.start()
        return c

    def fwd_start(s, lt_now):
        lt_send[s] = lt_now
        c1 = scan_start(s, st_own, st_send, st_recv, st_ss, st_rs)
        c2 = seq_copy(lt_send.at[s], lt_recv.at[s], lt_ss.at[s], lt_rs.at[s], s)
        c2.start()
        return (c1, c2)

    def fwd_finish(s, cs, lt_now, lp_now):
        for c in cs:
            c.wait()
        b = bit_of(s).astype(F32)
        lt_in = lt_recv[s]
        lt_hist.append((lt_now, lt_in))
        f_pre = jnp.exp(lp_now) * b
        f_own = jnp.exp((1.0 - b) * lt_in)
        f_in = jnp.exp(b * lt_now)
        for h in range(heads):
            t_in = st_recv[s, h].astype(F32)
            st_pre[h] = st_pre[h] + f_pre[h : h + 1, :] * t_in
            if s < nb - 1:
                st_own[h] = st_own[h] * f_own[h : h + 1, :] + t_in * f_in[h : h + 1, :]
        return lt_now + lt_in, lp_now + b * lt_in

    cs = fwd_start(0, lt_tile)

    loads[4].wait()
    x = dot(tok[...], wsq[...])
    for h in range(heads):
        sq_s[h] = unit(x[:, h * hs : (h + 1) * hs]).astype(BF16)
    loads[5].wait()
    q_s[...] = dot(tok[...], wq[...]).astype(BF16)
    k_pos = lax.broadcasted_iota(jnp.int32, (rows, rows), 0)
    q_pos = lax.broadcasted_iota(jnp.int32, (rows, rows), 1)
    allowed = k_pos <= q_pos

    def intra(h):
        a = dot_t(sk_s[h], sq_s[h])
        gap = crow_ref[h : h + 1, :] - ccol_ref[:, h : h + 1]
        mixed = (a * jnp.exp(jnp.where(allowed, gap, NEG_FILL))).astype(BF16)
        mix[h] = mixed
        out_t[h] = dot(svt[h], mixed)

    for h in range(heads // 2):
        intra(h)

    lt_tile, lp_tile = fwd_finish(0, cs, lt_tile, lp_tile)
    if nb > 1:
        cs = fwd_start(1, lt_tile)

    for c in part_copies:
        c.wait()
    lat[me] = jnp.concatenate([parts[i] for i in range(nt)], axis=1)
    half = rows // 2
    orders = [list(range(1, nb)) + [0], list(range(nb - 1, 0, -1)) + [0]]

    def lat_start(s):
        out = []
        for side in range(2):
            b = orders[side][s]
            for o, off in enumerate(combos(orders[side][:s])):
                view = lat.at[flip(me, off), pl.ds(side * half, half), :]
                slot = (1 << s) - 1 + o
                c = seq_copy(view, view, lat_ss.at[side, slot], lat_rs.at[side, slot], b)
                c.start()
                out.append(c)
        return out

    lat_copies = lat_start(0)

    for h in range(heads // 2, heads):
        intra(h)
    loads[6].wait()
    loads[7].wait()
    wvut[...] = wvu[...].astype(F32).T.astype(BF16)

    def attend(j, masked, first):
        block = lat[j]
        k_b = dot(block, wku[...]).astype(BF16)
        v_t = dot_t(wvut[...], block).astype(BF16)
        for h in range(heads):
            s = dot_t(k_b[:, h * hs : (h + 1) * hs], q_s[:, h * hs : (h + 1) * hs]) * scale
            if masked:
                s = jnp.where(allowed, s, NEG_FILL)
            top = jnp.max(s, axis=0, keepdims=True)
            if not first:
                old = m_s[h]
                top = jnp.maximum(old, top)
            p = jnp.exp2(s - top)
            total = jnp.sum(p, axis=0, keepdims=True)
            mixed = dot(v_t[h * hs : (h + 1) * hs, :], p.astype(BF16))
            if not first:
                f = jnp.exp2(old - top)
                total = total + l_s[h] * f
                mixed = mixed + acc_s[h] * f
            m_s[h] = top
            l_s[h] = total
            acc_s[h] = mixed

    for s in range(1, nb):
        lt_tile, lp_tile = fwd_finish(s, cs, lt_tile, lp_tile)
        if s < nb - 1:
            cs = fwd_start(s + 1, lt_tile)
        for c in lat_copies:
            c.wait()
        lat_copies = lat_start(s)
        if s == 1:
            attend(me, True, True)
    for h in range(heads):
        w = jnp.exp(crow_ref[h : h + 1, :])
        out_t[h] = out_t[h] + dot_t(st_pre[h].astype(BF16), sq_s[h]) * w
    for c in lat_copies:
        c.wait()

    def step(j, carry):
        attend(j, False, False)
        return carry

    lax.fori_loop(0, me, step, 0)

    total_rows = n * rows
    loss = jnp.zeros((8, 128), F32)
    for h in range(heads):
        c_h = crow_ref[h : h + 1, :]
        teach = (acc_s[h] / l_s[h]).astype(BF16).astype(F32)
        tout_ref[:, h * hs : (h + 1) * hs] = teach.T.astype(BF16)
        miss = out_t[h] - teach
        sq = miss * miss
        loss = loss + jnp.broadcast_to(jnp.sum(jnp.sum(sq, axis=0, keepdims=True), axis=1, keepdims=True), (8, 128))
        g = miss * (1.0 / math.sqrt(total_rows))
        gt[h] = g.astype(BF16)
        bt_own[h] = dot((g * jnp.exp(c_h)).astype(BF16), sq_s[h])
        bt_suf[h] = jnp.zeros((hs, hs), F32)
    loss_s[...] = loss
    loss_copies = [
        tensor_copy(loss_s, loss_t.at[d - 1], lp_ss.at[d - 1], lp_rs.at[d - 1], d) for d in range(1, nt)
    ]
    bc = scan_start(0, bt_own, bt_send, bt_recv, bt_ss, bt_rs)
    for c in loss_copies:
        c.start()
    for h in range(heads):
        out_t[h] = dot_t(gt[h], mix[h])
    for s in range(nb):
        bc.wait()
        b = bit_of(s).astype(F32)
        lt_now, lt_in = lt_hist[s]
        f_suf = jnp.exp(lr_tile) * (1.0 - b)
        f_own = jnp.exp(b * lt_in)
        f_in = jnp.exp((1.0 - b) * lt_now)
        for h in range(heads):
            t_in = bt_recv[s, h].astype(F32)
            if s < nb - 1:
                bt_own[h] = bt_own[h] * f_own[h : h + 1, :] + t_in * f_in[h : h + 1, :]
            bt_suf[h] = bt_suf[h] + f_suf[h : h + 1, :] * t_in
        lr_tile = lr_tile + (1.0 - b) * lt_in
        if s < nb - 1:
            bc = scan_start(s + 1, bt_own, bt_send, bt_recv, bt_ss, bt_rs)
    for h in range(heads):
        c_h = crow_ref[h : h + 1, :]
        w = jnp.exp(c_h[:, rows - 1 : rows] - c_h)
        vg = out_t[h] + dot_t(bt_suf[h].astype(BF16), sk_s[h]) * w
        vgt[h * hs : (h + 1) * hs, :] = vg.astype(BF16)
    for c in loss_copies:
        c.wait()
    for d in range(nt - 1):
        loss = loss + loss_t[d]

    cols = heads * hs
    width = wg_ref.shape[0]
    ch = cols // 2
    wg_orders = [list(range(nb)), [0] + list(range(nb - 1, 0, -1))]

    def product(off):
        at = pl.multiple_of(flip(me, off) * width, width)
        return dot(vgt[...], tok[:, pl.ds(at, width)])

    for s in range(nb):
        copies = []
        live = []
        for side in range(2):
            b = wg_orders[side][s]
            rest = combos(wg_orders[side][s + 1 :])
            base = n - (n >> s)
            live.append((b, rest, base))
        if s == 0:
            b, rest, base = live[0]
            for c_off in rest:
                slot = base + rest.index(c_off)
                y = product(c_off | (1 << b)).astype(BF16)
                for side in range(2):
                    sl = base + live[side][1].index(c_off)
                    wg_send[side, sl] = y[side * ch : (side + 1) * ch]
                    c = seq_copy(wg_send.at[side, sl], wg_recv.at[side, sl], wg_ss.at[side, sl], wg_rs.at[side, sl], b)
                    c.start()
                    copies.append(c)
        else:
            for i in range(max(len(live[0][1]), 1)):
                for side in range(2):
                    b, rest, base = live[side]
                    sl = base + i
                    wg_send[side, sl] = wg_acc[side, (rest[i] | (1 << b)) >> 1].astype(BF16)
                    c = seq_copy(wg_send.at[side, sl], wg_recv.at[side, sl], wg_ss.at[side, sl], wg_rs.at[side, sl], b)
                    c.start()
                    copies.append(c)
        loss_r[s] = loss
        lc = seq_copy(loss_r.at[s], loss_r2.at[s], lo_ss.at[s], lo_rs.at[s], s)
        lc.start()
        if s == 0:
            for c_off in live[0][1]:
                y = product(c_off)
                for side in range(2):
                    wg_acc[side, c_off >> 1] = y[side * ch : (side + 1) * ch]
        for c in copies:
            c.wait()
        lc.wait()
        loss = loss + loss_r2[s]
        for side in range(2):
            b, rest, base = live[side]
            for i, c_off in enumerate(rest):
                wg_acc[side, c_off >> 1] = wg_acc[side, c_off >> 1] + wg_recv[side, base + i].astype(F32)
    for side in range(2):
        wg_ref[:, side * ch : (side + 1) * ch] = wg_acc[side, 0].T
    loss_ref[...] = loss


def per_device(
    tokens, w_latent, w_query, w_key_up, w_value_up, w_stu_query, w_stu_key, w_stu_value, forget
):
    n, nt = lax.axis_size("seq"), lax.axis_size("tensor")
    rows, model = tokens.shape
    heads = forget.shape[1]
    cols = w_query.shape[1]
    hs = cols // heads
    lat_part = w_latent.shape[1]
    lat_all = w_key_up.shape[0]
    width = model // n
    nb = n.bit_length() - 1
    ccol = jnp.cumsum(forget, axis=0)
    crow = ccol.T
    vm = pltpu.VMEM
    dma = pltpu.SemaphoreType.DMA
    any_spec = pl.BlockSpec(memory_space=pl.ANY)
    vm_spec = pl.BlockSpec(memory_space=pltpu.VMEM)
    ch = cols // 2
    tout, loss, wg = pl.pallas_call(
        functools.partial(kernel, n, nt, heads, hs, rows),
        out_shape=(
            jax.ShapeDtypeStruct((rows, cols), BF16),
            jax.ShapeDtypeStruct((8, 128), F32),
            jax.ShapeDtypeStruct((width, cols), F32),
        ),
        in_specs=[any_spec] * 8 + [vm_spec] * 2,
        out_specs=(vm_spec,) * 3,
        scratch_shapes=[
            vm((rows, model), BF16), vm((model, lat_part), BF16), vm((model, cols), BF16),
            vm((lat_all, cols), BF16), vm((lat_all, cols), BF16), vm((model, cols), BF16),
            vm((model, cols), BF16), vm((model, cols), BF16), vm((cols, lat_all), BF16),
            vm((nt, rows, lat_part), BF16), vm((n, rows, lat_all), BF16),
            vm((rows, cols), BF16), vm((heads, rows, hs), BF16), vm((heads, rows, hs), BF16),
            vm((heads, hs, rows), BF16), vm((heads, rows, rows), BF16), vm((heads, hs, rows), F32),
            vm((heads, 1, rows), F32), vm((heads, 1, rows), F32), vm((heads, hs, rows), F32),
            vm((heads, hs, hs), F32), vm((heads, hs, hs), F32),
            vm((nb, heads, hs, hs), BF16), vm((nb, heads, hs, hs), BF16),
            vm((nb, 8, 128), F32), vm((nb, 8, 128), F32),
            vm((heads, hs, rows), BF16), vm((heads, hs, hs), F32), vm((heads, hs, hs), F32),
            vm((nb, heads, hs, hs), BF16), vm((nb, heads, hs, hs), BF16), vm((cols, rows), BF16),
            vm((2, n // 2, ch, width), F32), vm((2, n - 1, ch, width), BF16), vm((2, n - 1, ch, width), BF16),
            vm((nt - 1, 8, 128), F32), vm((nb, 8, 128), F32), vm((8, 128), F32), vm((nb, 8, 128), F32),
            dma((8,)), dma((nt - 1,)), dma((nt - 1,)), dma((2, n - 1)), dma((2, n - 1)),
            dma((nb,)), dma((nb,)), dma((nb,)), dma((nb,)), dma((nb,)), dma((nb,)),
            dma((2, n - 1)), dma((2, n - 1)), dma((nb,)), dma((nb,)), dma((nt - 1,)), dma((nt - 1,)),
        ],
        compiler_params=pltpu.CompilerParams(
            collective_id=0, has_side_effects=True, vmem_limit_bytes=60 * 1024 * 1024
        ),
    )(tokens, w_latent, w_query, w_key_up, w_value_up, w_stu_query, w_stu_key, w_stu_value, crow, ccol)
    count = 2.0 * n * rows * cols * nt
    return (tout, loss[0, 0] / count, wg)


def solution(mesh):
    return jax.shard_map(
        per_device,
        mesh=mesh,
        in_specs=(
            P("seq", None),
            P(None, "tensor"),
            P(None, "tensor"),
            P(None, "tensor"),
            P(None, "tensor"),
            P(None, "tensor"),
            P(None, "tensor"),
            P(None, "tensor"),
            P("seq", "tensor"),
        ),
        out_specs=(P("seq", "tensor"), P(), P("seq", "tensor")),
        check_vma=False,
    )
```

```python
import functools
import math

import jax
import jax.numpy as jnp
from jax import lax
from jax.experimental import pallas as pl
from jax.experimental.pallas import tpu as pltpu
from jax.sharding import PartitionSpec as P

NEG_FILL = -1e30
EPSILON = 1e-06
MESH = pl.DeviceIdType.MESH
F32, BF16 = jnp.float32, jnp.bfloat16


def flip(index, mask):
    out, bit = index, 0
    while (1 << bit) <= mask:
        if (mask >> bit) & 1:
            out = out + (1 << bit) * (1 - 2 * ((index // (1 << bit)) % 2))
        bit += 1
    return out


def combos(bits):
    out = [0]
    for b in bits:
        out = out + [o | (1 << b) for o in out]
    return out


def dot_t(a, b):
    return lax.dot_general(a, b, (((1,), (1,)), ((), ())), preferred_element_type=F32)


def dot(a, b):
    return jnp.dot(a, b, preferred_element_type=F32)


def kernel(
    n, nt, heads, hs, rows,
    tok_h, wl_h, wq_h, wku_h, wvu_h, wsq_h, wsk_h, wsv_h, crow_ref, ccol_ref,
    tout_ref, loss_ref, wg_ref,
    tok, wl, wq, wku, wvu, wsq, wsk, wsv, wvut,
    parts, lat, q_s, sq_s, sk_s, svt, mix, out_t, m_s, l_s, acc_s,
    st_own, st_pre, st_send, st_recv, lt_send, lt_recv,
    gt, bt_own, bt_suf, bt_send, bt_recv, vgt,
    wg_acc, wg_send, wg_recv, loss_t, loss_r, loss_s, loss_r2,
    ld_sem, part_ss, part_rs, lat_ss, lat_rs, st_ss, st_rs, lt_ss, lt_rs, bt_ss, bt_rs,
    wg_ss, wg_rs, lo_ss, lo_rs, lp_ss, lp_rs,
):
    me = lax.axis_index("seq")
    tme = lax.axis_index("tensor")
    nb = n.bit_length() - 1
    scale = math.log2(math.e) / math.sqrt(hs)

    def bit_of(b):
        return (me // (1 << b)) % 2

    loads = [
        pltpu.make_async_copy(src, dst, ld_sem.at[i])
        for i, (src, dst) in enumerate(
            [(tok_h, tok), (wl_h, wl), (wsk_h, wsk), (wsv_h, wsv), (wsq_h, wsq), (wq_h, wq), (wku_h, wku), (wvu_h, wvu)]
        )
    ]
    for load in loads:
        load.start()

    barrier = pltpu.get_barrier_semaphore()
    for b in range(nb):
        pl.semaphore_signal(barrier, inc=1, device_id=(flip(me, 1 << b), tme), device_id_type=MESH)
    for d in range(1, nt):
        pl.semaphore_signal(barrier, inc=1, device_id=(me, (tme + d) % nt), device_id_type=MESH)
    pl.semaphore_wait(barrier, nb + nt - 1)

    def seq_copy(src, dst, ss, rs, b):
        return pltpu.make_async_remote_copy(
            src_ref=src, dst_ref=dst, send_sem=ss, recv_sem=rs,
            device_id=(flip(me, 1 << b), tme), device_id_type=MESH,
        )

    def tensor_copy(src, dst, ss, rs, d):
        return pltpu.make_async_remote_copy(
            src_ref=src, dst_ref=dst, send_sem=ss, recv_sem=rs,
            device_id=(me, (tme + d) % nt), device_id_type=MESH,
        )

    pending = []

    loads[0].wait()
    loads[1].wait()
    parts[tme] = dot(tok[...], wl[...]).astype(BF16)
    part_copies = [
        tensor_copy(parts.at[tme], parts.at[tme], part_ss.at[d - 1], part_rs.at[d - 1], d) for d in range(1, nt)
    ]
    for c in part_copies:
        c.start()

    def unit(x):
        return x * lax.rsqrt(jnp.sum(x * x, axis=-1, keepdims=True) + EPSILON)

    loads[2].wait()
    x = dot(tok[...], wsk[...])
    for h in range(heads):
        sk_s[h] = unit(x[:, h * hs : (h + 1) * hs]).astype(BF16)
    loads[3].wait()
    x = dot(tok[...], wsv[...])
    lt = []
    for h in range(heads):
        xt = x[:, h * hs : (h + 1) * hs].T
        svt[h] = xt.astype(BF16)
        c_h = crow_ref[h : h + 1, :]
        end = c_h[:, rows - 1 : rows]
        st_own[h] = dot((xt * jnp.exp(end - c_h)).astype(BF16), sk_s[h])
        st_pre[h] = jnp.zeros((hs, hs), F32)
        lt.append(jnp.broadcast_to(end, (1, 128)))
    zero_row = jnp.zeros((1, 128), F32)
    lt_tile = jnp.concatenate(lt + [zero_row] * (8 - heads), axis=0)
    lp_tile = jnp.zeros((8, 128), F32)
    lr_tile = jnp.zeros((8, 128), F32)
    lt_hist = []

    def scan_start(s, own, send, recv, ss, rs):
        for h in range(heads):
            send[s, h] = own[h].astype(BF16)
        c = seq_copy(send.at[s], recv.at[s], ss.at[s], rs.at[s], s)
        c.start()
        return c

    def fwd_start(s, lt_now):
        lt_send[s] = lt_now
        c1 = scan_start(s, st_own, st_send, st_recv, st_ss, st_rs)
        c2 = seq_copy(lt_send.at[s], lt_recv.at[s], lt_ss.at[s], lt_rs.at[s], s)
        c2.start()
        return (c1, c2)

    def fwd_finish(s, cs, lt_now, lp_now):
        for c in cs:
            c.wait()
        b = bit_of(s).astype(F32)
        lt_in = lt_recv[s]
        lt_hist.append((lt_now, lt_in))
        f_pre = jnp.exp(lp_now) * b
        f_own = jnp.exp((1.0 - b) * lt_in)
        f_in = jnp.exp(b * lt_now)
        for h in range(heads):
            t_in = st_recv[s, h].astype(F32)
            st_pre[h] = st_pre[h] + f_pre[h : h + 1, :] * t_in
            if s < nb - 1:
                st_own[h] = st_own[h] * f_own[h : h + 1, :] + t_in * f_in[h : h + 1, :]
        return lt_now + lt_in, lp_now + b * lt_in

    cs = fwd_start(0, lt_tile)

    loads[4].wait()
    x = dot(tok[...], wsq[...])
    for h in range(heads):
        sq_s[h] = unit(x[:, h * hs : (h + 1) * hs]).astype(BF16)
    loads[5].wait()
    q_s[...] = dot(tok[...], wq[...]).astype(BF16)
    k_pos = lax.broadcasted_iota(jnp.int32, (rows, rows), 0)
    q_pos = lax.broadcasted_iota(jnp.int32, (rows, rows), 1)
    allowed = k_pos <= q_pos

    def intra(h):
        a = dot_t(sk_s[h], sq_s[h])
        gap = crow_ref[h : h + 1, :] - ccol_ref[:, h : h + 1]
        mixed = (a * jnp.exp(jnp.where(allowed, gap, NEG_FILL))).astype(BF16)
        mix[h] = mixed
        out_t[h] = dot(svt[h], mixed)

    for h in range(heads // 2):
        intra(h)

    lt_tile, lp_tile = fwd_finish(0, cs, lt_tile, lp_tile)
    if nb > 1:
        cs = fwd_start(1, lt_tile)

    for c in part_copies:
        c.wait()
    lat[me] = jnp.concatenate([parts[i] for i in range(nt)], axis=1)
    half = rows // 2
    orders = [list(range(1, nb)) + [0], list(range(nb - 1, 0, -1)) + [0]]

    core_copies = []

    def lat_copy(side, off, slot, b):
        view = lat.at[flip(me, off), pl.ds(side * half, half), :]
        c = seq_copy(view, view, lat_ss.at[side, slot], lat_rs.at[side, slot], b)
        c.start()
        return c

    def lat_start(s):
        out = []
        for side in range(2):
            have = combos(orders[side][:s])
            if s < nb - 1:
                b = orders[side][s]
                out += [lat_copy(side, off, (1 << s) - 1 + o, b) for o, off in enumerate(have)]
            for o in range((1 << s) // 2, 1 << s):
                core_copies.append(lat_copy(side, have[o], (1 << (nb - 1)) - 1 + o, 0))
        return out

    lat_copies = lat_start(0)

    for h in range(heads // 2, heads):
        intra(h)
    loads[6].wait()
    loads[7].wait()
    wvut[...] = wvu[...].astype(F32).T.astype(BF16)

    def attend(j, masked, first):
        block = lat[j]
        k_b = dot(block, wku[...]).astype(BF16)
        v_t = dot_t(wvut[...], block).astype(BF16)
        for h in range(heads):
            s = dot_t(k_b[:, h * hs : (h + 1) * hs], q_s[:, h * hs : (h + 1) * hs]) * scale
            if masked:
                s = jnp.where(allowed, s, NEG_FILL)
            top = jnp.max(s, axis=0, keepdims=True)
            if not first:
                old = m_s[h]
                top = jnp.maximum(old, top)
            p = jnp.exp2(s - top)
            total = jnp.sum(p, axis=0, keepdims=True)
            mixed = dot(v_t[h * hs : (h + 1) * hs, :], p.astype(BF16))
            if not first:
                f = jnp.exp2(old - top)
                total = total + l_s[h] * f
                mixed = mixed + acc_s[h] * f
            m_s[h] = top
            l_s[h] = total
            acc_s[h] = mixed

    for s in range(1, nb):
        lt_tile, lp_tile = fwd_finish(s, cs, lt_tile, lp_tile)
        if s < nb - 1:
            cs = fwd_start(s + 1, lt_tile)
        for c in lat_copies:
            c.wait()
        lat_copies = lat_start(s)
        if s == 1:
            attend(me, True, True)
    for h in range(heads):
        w = jnp.exp(crow_ref[h : h + 1, :])
        out_t[h] = out_t[h] + dot_t(st_pre[h].astype(BF16), sq_s[h]) * w
    for c in lat_copies:
        c.wait()
    parity = me % 2

    def near_step(k, carry):
        attend(2 * k + parity, False, False)
        return carry

    def far_step(k, carry):
        attend(2 * k + 1 - parity, False, False)
        return carry

    lax.fori_loop(0, me // 2, near_step, 0)
    for c in core_copies:
        c.wait()
    lax.fori_loop(0, (me + 1) // 2, far_step, 0)

    total_rows = n * rows
    loss = jnp.zeros((8, 128), F32)
    for h in range(heads):
        c_h = crow_ref[h : h + 1, :]
        teach = (acc_s[h] / l_s[h]).astype(BF16).astype(F32)
        tout_ref[:, h * hs : (h + 1) * hs] = teach.T.astype(BF16)
        miss = out_t[h] - teach
        sq = miss * miss
        loss = loss + jnp.broadcast_to(jnp.sum(jnp.sum(sq, axis=0, keepdims=True), axis=1, keepdims=True), (8, 128))
        g = miss * (1.0 / math.sqrt(total_rows))
        gt[h] = g.astype(BF16)
        bt_own[h] = dot((g * jnp.exp(c_h)).astype(BF16), sq_s[h])
        bt_suf[h] = jnp.zeros((hs, hs), F32)
    loss_s[...] = loss
    loss_copies = [
        tensor_copy(loss_s, loss_t.at[d - 1], lp_ss.at[d - 1], lp_rs.at[d - 1], d) for d in range(1, nt)
    ]
    bc = scan_start(0, bt_own, bt_send, bt_recv, bt_ss, bt_rs)
    for c in loss_copies:
        c.start()
    for h in range(heads):
        out_t[h] = dot_t(gt[h], mix[h])
    for s in range(nb):
        bc.wait()
        b = bit_of(s).astype(F32)
        lt_now, lt_in = lt_hist[s]
        f_suf = jnp.exp(lr_tile) * (1.0 - b)
        f_own = jnp.exp(b * lt_in)
        f_in = jnp.exp((1.0 - b) * lt_now)
        for h in range(heads):
            t_in = bt_recv[s, h].astype(F32)
            if s < nb - 1:
                bt_own[h] = bt_own[h] * f_own[h : h + 1, :] + t_in * f_in[h : h + 1, :]
            bt_suf[h] = bt_suf[h] + f_suf[h : h + 1, :] * t_in
        lr_tile = lr_tile + (1.0 - b) * lt_in
        if s < nb - 1:
            bc = scan_start(s + 1, bt_own, bt_send, bt_recv, bt_ss, bt_rs)
    for h in range(heads):
        c_h = crow_ref[h : h + 1, :]
        w = jnp.exp(c_h[:, rows - 1 : rows] - c_h)
        vg = out_t[h] + dot_t(bt_suf[h].astype(BF16), sk_s[h]) * w
        vgt[h * hs : (h + 1) * hs, :] = vg.astype(BF16)
    for c in loss_copies:
        c.wait()
    for d in range(nt - 1):
        loss = loss + loss_t[d]

    cols = heads * hs
    width = wg_ref.shape[0]
    ch = cols // 2
    wg_orders = [list(range(nb)), [0] + list(range(nb - 1, 0, -1))]

    def product(off):
        at = pl.multiple_of(flip(me, off) * width, width)
        return dot(vgt[...], tok[:, pl.ds(at, width)])

    for s in range(nb):
        copies = []
        live = []
        for side in range(2):
            b = wg_orders[side][s]
            rest = combos(wg_orders[side][s + 1 :])
            base = n - (n >> s)
            live.append((b, rest, base))
        if s == 0:
            b, rest, base = live[0]
            for c_off in rest:
                slot = base + rest.index(c_off)
                y = product(c_off | (1 << b)).astype(BF16)
                for side in range(2):
                    sl = base + live[side][1].index(c_off)
                    wg_send[side, sl] = y[side * ch : (side + 1) * ch]
                    c = seq_copy(wg_send.at[side, sl], wg_recv.at[side, sl], wg_ss.at[side, sl], wg_rs.at[side, sl], b)
                    c.start()
                    copies.append(c)
        else:
            for i in range(max(len(live[0][1]), 1)):
                for side in range(2):
                    b, rest, base = live[side]
                    sl = base + i
                    wg_send[side, sl] = wg_acc[side, (rest[i] | (1 << b)) >> 1].astype(BF16)
                    c = seq_copy(wg_send.at[side, sl], wg_recv.at[side, sl], wg_ss.at[side, sl], wg_rs.at[side, sl], b)
                    c.start()
                    copies.append(c)
        loss_r[s] = loss
        lc = seq_copy(loss_r.at[s], loss_r2.at[s], lo_ss.at[s], lo_rs.at[s], s)
        lc.start()
        if s == 0:
            for c_off in live[0][1]:
                y = product(c_off)
                for side in range(2):
                    wg_acc[side, c_off >> 1] = y[side * ch : (side + 1) * ch]
        for c in copies:
            c.wait()
        lc.wait()
        loss = loss + loss_r2[s]
        for side in range(2):
            b, rest, base = live[side]
            for i, c_off in enumerate(rest):
                wg_acc[side, c_off >> 1] = wg_acc[side, c_off >> 1] + wg_recv[side, base + i].astype(F32)
    for side in range(2):
        wg_ref[:, side * ch : (side + 1) * ch] = wg_acc[side, 0].T
    loss_ref[...] = loss


def per_device(
    tokens, w_latent, w_query, w_key_up, w_value_up, w_stu_query, w_stu_key, w_stu_value, forget
):
    n, nt = lax.axis_size("seq"), lax.axis_size("tensor")
    rows, model = tokens.shape
    heads = forget.shape[1]
    cols = w_query.shape[1]
    hs = cols // heads
    lat_part = w_latent.shape[1]
    lat_all = w_key_up.shape[0]
    width = model // n
    nb = n.bit_length() - 1
    ccol = jnp.cumsum(forget, axis=0)
    crow = ccol.T
    vm = pltpu.VMEM
    dma = pltpu.SemaphoreType.DMA
    any_spec = pl.BlockSpec(memory_space=pl.ANY)
    vm_spec = pl.BlockSpec(memory_space=pltpu.VMEM)
    ch = cols // 2
    tout, loss, wg = pl.pallas_call(
        functools.partial(kernel, n, nt, heads, hs, rows),
        out_shape=(
            jax.ShapeDtypeStruct((rows, cols), BF16),
            jax.ShapeDtypeStruct((8, 128), F32),
            jax.ShapeDtypeStruct((width, cols), F32),
        ),
        in_specs=[any_spec] * 8 + [vm_spec] * 2,
        out_specs=(vm_spec,) * 3,
        scratch_shapes=[
            vm((rows, model), BF16), vm((model, lat_part), BF16), vm((model, cols), BF16),
            vm((lat_all, cols), BF16), vm((lat_all, cols), BF16), vm((model, cols), BF16),
            vm((model, cols), BF16), vm((model, cols), BF16), vm((cols, lat_all), BF16),
            vm((nt, rows, lat_part), BF16), vm((n, rows, lat_all), BF16),
            vm((rows, cols), BF16), vm((heads, rows, hs), BF16), vm((heads, rows, hs), BF16),
            vm((heads, hs, rows), BF16), vm((heads, rows, rows), BF16), vm((heads, hs, rows), F32),
            vm((heads, 1, rows), F32), vm((heads, 1, rows), F32), vm((heads, hs, rows), F32),
            vm((heads, hs, hs), F32), vm((heads, hs, hs), F32),
            vm((nb, heads, hs, hs), BF16), vm((nb, heads, hs, hs), BF16),
            vm((nb, 8, 128), F32), vm((nb, 8, 128), F32),
            vm((heads, hs, rows), BF16), vm((heads, hs, hs), F32), vm((heads, hs, hs), F32),
            vm((nb, heads, hs, hs), BF16), vm((nb, heads, hs, hs), BF16), vm((cols, rows), BF16),
            vm((2, n // 2, ch, width), F32), vm((2, n - 1, ch, width), BF16), vm((2, n - 1, ch, width), BF16),
            vm((nt - 1, 8, 128), F32), vm((nb, 8, 128), F32), vm((8, 128), F32), vm((nb, 8, 128), F32),
            dma((8,)), dma((nt - 1,)), dma((nt - 1,)), dma((2, n - 1)), dma((2, n - 1)),
            dma((nb,)), dma((nb,)), dma((nb,)), dma((nb,)), dma((nb,)), dma((nb,)),
            dma((2, n - 1)), dma((2, n - 1)), dma((nb,)), dma((nb,)), dma((nt - 1,)), dma((nt - 1,)),
        ],
        compiler_params=pltpu.CompilerParams(
            collective_id=0, has_side_effects=True, vmem_limit_bytes=60 * 1024 * 1024
        ),
    )(tokens, w_latent, w_query, w_key_up, w_value_up, w_stu_query, w_stu_key, w_stu_value, crow, ccol)
    count = 2.0 * n * rows * cols * nt
    return (tout, loss[0, 0] / count, wg)


def solution(mesh):
    return jax.shard_map(
        per_device,
        mesh=mesh,
        in_specs=(
            P("seq", None),
            P(None, "tensor"),
            P(None, "tensor"),
            P(None, "tensor"),
            P(None, "tensor"),
            P(None, "tensor"),
            P(None, "tensor"),
            P(None, "tensor"),
            P("seq", "tensor"),
        ),
        out_specs=(P("seq", "tensor"), P(), P("seq", "tensor")),
        check_vma=False,
    )
```
